512 devices in a mesh: axial: 32 (over x, z), pitch: 8 (over y_lo, core), span: 2 (over y_hi).
Axes of the slice: x: 4, y: 8 (y_hi: 2, y_lo: 4; y = y_hi * 4 + y_lo), z: 8, core: 2. Of those that a mesh axis runs over, the one named last changes fastest.
Arguments:
- flow_state: float32 [5, 512, 64, 1024], P(None, 'axial', 'pitch', 'span')
- step_start: float32 [5, 512, 64, 1024], P(None, 'axial', 'pitch', 'span')
- lower_coef: float32 [16, 5, 512, 1024], P('pitch', None, 'axial', 'span')
- upper_coef: float32 [16, 5, 512, 1024], P('pitch', None, 'axial', 'span')
- partner_row: int32 [2, 512], P(None, 'axial'), may hold values from 0 to 511, as said below
- periodic_cells: int32 [2, 512], P(None, 'axial'), may hold values from 1 to 1024, as said below
- phase_angles: float32 [2], replicated, may hold values from -3.140625 to 3.140625
Outputs:
- next_state: float32 [5, 512, 64, 1024], P(None, 'axial', 'pitch', 'span')
The draws below stay inside these ranges and needn't reach their ends.
Inputs may be any that keep to these rules, and one draw needn't show every extreme that they name: `partner_row`: each row is a permutation of 0 .. 511 and row 1 is the inverse of row 0. Of the 16 rows of one axial device, in either row, exactly 1 name rows of each of 16 devices and none of any other device. `periodic_cells`: rows 128 up to 384 have 1 to 128 periodic cells; all other rows have 1024.
All inputs are finite; a program needn't handle non-finite values.
Results may differ from the reference program's by a relative error of at most 0.00005.
Values sent between devices are 32-bit elements; how exact they have to be, the bound alone decides.
A program may use at most 64 MiB of HBM per device.

```python
import jax
import jax.numpy as jnp
from jax import lax

NV = 5
NH = 16
CA = 16
CAP = 1
NA = 512
NP = 64
NS = 1024


def physical_field(key):
    subkeys = jax.random.split(key, 3)
    density = jax.random.uniform(subkeys[0], (NA, NP, NS), jnp.float32, 0.7, 1.3)
    velocity = jnp.clip(0.3 * jax.random.normal(subkeys[1], (3, NA, NP, NS), jnp.float32), -1.0, 1.0)
    pressure = jax.random.uniform(subkeys[2], (NA, NP, NS), jnp.float32, 0.7, 1.3)
    energy = pressure / 0.4 + 0.5 * density * jnp.sum(velocity * velocity, axis=0)
    return jnp.concatenate([density[None], density[None] * velocity, energy[None]], 0)


def harmonic_table(key):
    uniform_part = jax.random.uniform(key, (NH, NV, NA, NS), jnp.float32)
    term_ids = jnp.arange(NH)[:, None]
    var_ids = jnp.arange(NV)[None, :]
    mean_low = jnp.where(var_ids == 0, 0.9, jnp.where(var_ids == 4, 2.0, -0.5))
    mean_high = jnp.where(var_ids == 0, 1.3, jnp.where(var_ids == 4, 3.0, 0.5))
    wave_size = jnp.where(var_ids == 0, 0.04, 0.3)
    lower_end = jnp.where(term_ids == 0, mean_low, -wave_size)
    upper_end = jnp.where(term_ids == 0, mean_high, wave_size)
    return lower_end[:, :, None, None] + (upper_end - lower_end)[:, :, None, None] * uniform_part


def draw_flow_state(key, part):
    return physical_field(jax.random.fold_in(key, 101))


def draw_step_start(key, part):
    return physical_field(jax.random.fold_in(key, 202))


def draw_lower_coef(key, part):
    return harmonic_table(jax.random.fold_in(key, 303))


def draw_upper_coef(key, part):
    return harmonic_table(jax.random.fold_in(key, 404))


def draw_partner_row(key, part):
    devices = NA // CA
    subkeys = jax.random.split(jax.random.fold_in(key, 505), 4)
    device_order = jax.random.permutation(subkeys[0], devices)
    group_count = CA // CAP
    chosen = jax.random.permutation(subkeys[1], devices)[:group_count]
    shift_values = jax.random.permutation(subkeys[2], jnp.repeat(chosen, CAP))
    scores = jax.random.randint(subkeys[3], (devices, CA), 0, 1 << 20) * CA + jnp.arange(CA)[None, :]
    offsets_table = jnp.argsort(scores, axis=1).astype(jnp.int32)
    source_ids = jnp.arange(devices)[:, None]
    row_ids = jnp.arange(CA)[None, :]
    target = (device_order[source_ids] + shift_values[row_ids]) % devices
    target_offset = offsets_table[target, row_ids]
    forward = (target * CA + target_offset).reshape(NA).astype(jnp.int32)
    inverse = jnp.zeros((NA,), jnp.int32).at[forward].set(jnp.arange(NA, dtype=jnp.int32))
    return jnp.stack([forward, inverse]).astype(jnp.int32)


def draw_periodic_cells(key, part):
    gaps = jax.random.randint(jax.random.fold_in(key, 606), (2, NA), 1, NS // 8 + 1)
    row_ids = jnp.arange(NA)[None, :]
    blade = (row_ids >= NA // 4) & (row_ids < 3 * NA // 4)
    return jnp.where(blade, gaps, NS).astype(jnp.int32)


def setup_inputs(seed: int = 0) -> dict:
    key_list = jax.random.split(jax.random.key(seed), 8)
    return {
        "flow_state": draw_flow_state(jax.random.fold_in(key_list[7], 71), 0),
        "step_start": draw_step_start(jax.random.fold_in(key_list[7], 71), 0),
        "lower_coef": draw_lower_coef(jax.random.fold_in(key_list[7], 71), 0),
        "upper_coef": draw_upper_coef(jax.random.fold_in(key_list[7], 71), 0),
        "partner_row": draw_partner_row(jax.random.fold_in(key_list[7], 71), 0),
        "periodic_cells": draw_periodic_cells(jax.random.fold_in(key_list[7], 71), 0),
        "phase_angles": jnp.clip(jax.random.uniform(key_list[6], (2,), jnp.float32, -3.140625, 3.140625), -3.140625, 3.140625),
    }


DISSIPATION = 0.25
SECTION_STEP = 0.5


def euler_flux(fields, direction):
    density = fields[0]
    velocity = fields[direction] / density
    pressure = 0.4 * (fields[4] - 0.5 * (fields[1] * fields[1] + fields[2] * fields[2] + fields[3] * fields[3]) / density)
    components = [fields[direction], fields[1] * velocity, fields[2] * velocity, fields[3] * velocity, (fields[4] + pressure) * velocity]
    components[direction] = components[direction] + pressure
    return jnp.stack(components)


def section_update(center, start_state, lows, highs):
    residual_sum = jnp.zeros_like(center)
    for direction in range(3):
        lower_side = lows[direction]
        upper_side = highs[direction]
        residual_sum = residual_sum - 0.5 * (euler_flux(upper_side, direction + 1) - euler_flux(lower_side, direction + 1)) + DISSIPATION * (upper_side + lower_side - 2.0 * center)
    return start_state + SECTION_STEP * residual_sum


def term_basis(phase_value, term_ids):
    harmonic = ((term_ids + 1) // 2).astype(phase_value.dtype)
    return jnp.where((term_ids % 2 == 0) & (term_ids > 0), jnp.sin(harmonic * phase_value), jnp.cos(harmonic * phase_value))


def reference(flow_state, step_start, lower_coef, upper_coef, partner_row, periodic_cells, phase_angles):
    term_ids = jnp.arange(NH, dtype=jnp.int32)
    lower_basis = term_basis(phase_angles[0], term_ids)
    upper_basis = term_basis(phase_angles[1], term_ids)
    lower_values = jnp.einsum('h,hvrs->vrs', lower_basis, upper_coef[:, :, partner_row[0], :], precision=lax.Precision.HIGHEST)
    upper_values = jnp.einsum('h,hvrs->vrs', upper_basis, lower_coef[:, :, partner_row[1], :], precision=lax.Precision.HIGHEST)
    mirror_sign = jnp.array([1.0, 1.0, -1.0, 1.0, 1.0], dtype=flow_state.dtype)[:, None, None]
    span_pos = jnp.arange(NS, dtype=jnp.int32)
    lower_open = span_pos[None, :] >= NS - periodic_cells[0][:, None]
    upper_open = span_pos[None, :] >= NS - periodic_cells[1][:, None]
    lower_ghost = jnp.where(lower_open[None], lower_values, flow_state[:, :, 0, :] * mirror_sign)
    upper_ghost = jnp.where(upper_open[None], upper_values, flow_state[:, :, NP - 1, :] * mirror_sign)
    axial_low = jnp.concatenate([flow_state[:, :1], flow_state[:, :-1]], 1)
    axial_high = jnp.concatenate([flow_state[:, 1:], flow_state[:, -1:]], 1)
    pitch_low = jnp.concatenate([lower_ghost[:, :, None, :], flow_state[:, :, :-1]], 2)
    pitch_high = jnp.concatenate([flow_state[:, :, 1:], upper_ghost[:, :, None, :]], 2)
    span_low = jnp.roll(flow_state, 1, 3)
    span_high = jnp.roll(flow_state, -1, 3)
    return section_update(flow_state, step_start, (axial_low, pitch_low, span_low), (axial_high, pitch_high, span_high))
```

```python
import functools

import jax
import jax.numpy as jnp
from jax import lax
from jax.experimental import pallas as pl
from jax.experimental.pallas import tpu as pltpu
from jax.sharding import PartitionSpec as P

MESH = pl.DeviceIdType.MESH
LANES = 128


def pressure_of(u):
    kinetic = 0.5 * (u[1] * u[1] + u[2] * u[2] + u[3] * u[3]) / u[0]
    return 0.4 * (u[4] - kinetic)


def flux_of(u, pressure, direction):
    velocity = u[direction] / u[0]
    parts = [u[direction], u[1] * velocity, u[2] * velocity, u[3] * velocity, (u[4] + pressure) * velocity]
    parts[direction] = parts[direction] + pressure
    return parts


def as_previous(u, flux):
    return [0.125 * a + 0.25 * f for a, f in zip(u, flux)]


def as_next(u, flux):
    return [0.125 * a - 0.25 * f for a, f in zip(u, flux)]


def kernel(
    sizes, flow, step, lower_coef, upper_coef, basis, partner, periodic, acc_out, delta_out,
    fx, sx, coef, part, rx_core, rx_chain, total, slots, recv, edge, halo, halo_in, span_tx, span_rx, span_in,
    out_v, ghost, delta, table,
    load_sem, core_send, core_recv, chain_send, chain_recv, row_send, row_recv,
    axial_send, axial_recv, pitch_send, pitch_recv, span_send, span_recv, store_sem, delta_sem,
):
    n_axial, n_pitch, n_span, n_var, n_row, n_col, n_cell, n_term = sizes
    at = lax.axis_index("axial")
    pitch = lax.axis_index("pitch")
    span = lax.axis_index("span")
    chips = n_pitch // 2
    core = lax.rem(pitch, 2)
    chip = lax.div(pitch, 2)
    place = jnp.where(core == 0, chips - 1 - chip, chip)
    step_to = jnp.where(core == 0, pitch - 2, pitch + 2)
    is_end = place == chips - 1
    mate = pitch + 1 - 2 * core
    beside = pitch - 1 + 2 * core
    has_beside = (beside >= 0) & (beside < n_pitch)
    tail = n_cell - LANES
    first_blade, end_blade = n_axial // 4, 3 * n_axial // 4

    def is_blade(a):
        return (a >= first_blade) & (a < end_blade)

    def load_coef(face):
        return [
            pltpu.make_async_copy(upper_coef, coef.at[0], load_sem.at[0]),
            pltpu.make_async_copy(lower_coef, coef.at[1], load_sem.at[1]),
        ][face]

    load_flow = pltpu.make_async_copy(flow, fx.at[:, pl.ds(1, n_row)], load_sem.at[2])
    load_step = pltpu.make_async_copy(step, sx, load_sem.at[3])
    load_coef(0).start()
    load_coef(1).start()
    load_flow.start()
    load_step.start()

    barrier = pltpu.get_barrier_semaphore()

    def greet(**where):
        pl.semaphore_signal(barrier, inc=1, device_id=where, device_id_type=MESH)

    greet(pitch=mate)

    @pl.when(has_beside)
    def _():
        greet(pitch=beside)

    @pl.when(pitch >= 2)
    def _():
        greet(pitch=pitch - 2)

    @pl.when(pitch < n_pitch - 2)
    def _():
        greet(pitch=pitch + 2)

    greet(span=1 - span)

    @pl.when(is_end)
    def _():
        @pl.loop(1, n_axial)
        def _(j):
            greet(axial=lax.rem(at + j, n_axial))

    @pl.when(jnp.logical_not(is_end) & (at > 0))
    def _():
        greet(axial=at - 1)

    @pl.when(jnp.logical_not(is_end) & (at < n_axial - 1))
    def _():
        greet(axial=at + 1)

    one = jnp.int32(1)
    zero = jnp.int32(0)
    near = jnp.where(at > 0, one, zero) + jnp.where(at < n_axial - 1, one, zero)
    greetings = (
        2
        + jnp.where(has_beside, one, zero)
        + jnp.where(pitch >= 2, one, zero)
        + jnp.where(pitch < n_pitch - 2, one, zero)
        + jnp.where(is_end, n_axial - 1, near)
    )

    def evaluate(face, v):
        value = basis[face, 0] * coef[face, 0, v]
        for t in range(1, n_term):
            value = value + basis[face, t] * coef[face, t, v]
        part[face, v] = value

    load_coef(0).wait()
    load_coef(1).wait()
    for v in range(n_var):
        evaluate(1 - core, v)

    pl.semaphore_wait(barrier, greetings)

    def core_copy(v):
        return pltpu.make_async_remote_copy(
            src_ref=part.at[1 - core, v], dst_ref=rx_core.at[v], send_sem=core_send.at[v], recv_sem=core_recv.at[v],
            device_id={"pitch": mate}, device_id_type=MESH)

    for v in range(n_var):
        core_copy(v).start()

    load_flow.wait()

    def axial_up():
        return pltpu.make_async_remote_copy(
            src_ref=fx.at[:, n_row], dst_ref=fx.at[:, 0], send_sem=axial_send.at[0], recv_sem=axial_recv.at[0],
            device_id={"axial": at + 1}, device_id_type=MESH)

    def axial_down():
        return pltpu.make_async_remote_copy(
            src_ref=fx.at[:, 1], dst_ref=fx.at[:, n_row + 1], send_sem=axial_send.at[1], recv_sem=axial_recv.at[1],
            device_id={"axial": at - 1}, device_id_type=MESH)

    @pl.when(at < n_axial - 1)
    def _():
        axial_up().start()

    @pl.when(at > 0)
    def _():
        axial_down().start()

    for v in range(n_var):
        evaluate(core, v)

    def chain_copy(v):
        return pltpu.make_async_remote_copy(
            src_ref=total.at[v], dst_ref=rx_chain.at[v], send_sem=chain_send.at[v], recv_sem=chain_recv.at[v],
            device_id={"pitch": step_to}, device_id_type=MESH)

    for v in range(n_var):
        core_copy(v).wait_recv()
        total[v] = part[core, v] + rx_core[v]

        @pl.when(place > 0)
        def _():
            chain_copy(v).wait_recv()
            total[v] = total[v] + rx_chain[v]

        @pl.when(jnp.logical_not(is_end))
        def _():
            chain_copy(v).start()

    def row_copy(target):
        return pltpu.make_async_remote_copy(
            src_ref=slots.at[target], dst_ref=recv.at[at], send_sem=row_send, recv_sem=row_recv,
            device_id={"axial": target}, device_id_type=MESH)

    def tip_copy(target):
        return pltpu.make_async_remote_copy(
            src_ref=slots.at[target, :, :, pl.ds(tail, LANES)], dst_ref=recv.at[at, :, :, pl.ds(tail, LANES)],
            send_sem=row_send, recv_sem=row_recv, device_id={"axial": target}, device_id_type=MESH)

    @pl.when(is_end)
    def _():
        @pl.loop(0, n_axial)
        def _(d):
            index = jnp.int32(0)
            for r in range(n_row):
                index = jnp.where(lax.div(partner[1 - core, r], n_row) == d, r, index)
            table[d] = index

        @pl.loop(1, n_axial)
        def _(j):
            target = lax.rem(at + j, n_axial)
            row = table[target]
            for v in range(n_var):
                slots[target, v] = total[v, pl.ds(row, 1), :]

            @pl.when(jnp.logical_not(is_blade(target)))
            def _():
                row_copy(target).start()

            @pl.when(is_blade(target) & (span == n_span - 1))
            def _():
                tip_copy(target).start()

        own = table[at]
        for v in range(n_var):
            recv[at, v] = total[v, pl.ds(own, 1), :]

    lane = lax.broadcasted_iota(jnp.int32, (n_col, LANES), 1)

    def pack(i, carry):
        low, high = carry
        for v in range(n_var):
            spot = v * n_row + i
            last = pltpu.roll(fx[v, i + 1, :, pl.ds(tail, LANES)], spot + 1, 1)
            first = pltpu.roll(fx[v, i + 1, :, pl.ds(0, LANES)], spot, 1)
            low = jnp.where(lane == spot, last, low)
            high = jnp.where(lane == spot, first, high)
            edge[0, v, pl.ds(i, 1), :] = fx[v, i + 1, pl.ds(0, 1), :]
            edge[1, v, pl.ds(i, 1), :] = fx[v, i + 1, pl.ds(n_col - 1, 1), :]
        return low, high

    blank = jnp.ones((n_col, LANES), jnp.float32)
    low, high = lax.fori_loop(0, n_row, pack, (blank, blank))
    span_tx[0] = low
    span_tx[1] = high

    span_copy = pltpu.make_async_remote_copy(
        src_ref=span_tx, dst_ref=span_rx, send_sem=span_send, recv_sem=span_recv,
        device_id={"span": 1 - span}, device_id_type=MESH)
    span_copy.start()

    def pitch_up():
        return pltpu.make_async_remote_copy(
            src_ref=edge.at[1], dst_ref=halo.at[0], send_sem=pitch_send.at[0], recv_sem=pitch_recv.at[0],
            device_id={"pitch": pitch + 1}, device_id_type=MESH)

    def pitch_down():
        return pltpu.make_async_remote_copy(
            src_ref=edge.at[0], dst_ref=halo.at[1], send_sem=pitch_send.at[1], recv_sem=pitch_recv.at[1],
            device_id={"pitch": pitch - 1}, device_id_type=MESH)

    @pl.when(pitch < n_pitch - 1)
    def _():
        pitch_up().start()

    @pl.when(pitch > 0)
    def _():
        pitch_down().start()

    @pl.when(at > 0)
    def _():
        axial_up().wait_recv()

    @pl.when(at == 0)
    def _():
        for v in range(n_var):
            fx[v, 0] = fx[v, 1]

    @pl.when(at < n_axial - 1)
    def _():
        axial_down().wait_recv()

    @pl.when(at == n_axial - 1)
    def _():
        for v in range(n_var):
            fx[v, n_row + 1] = fx[v, n_row]

    @pl.when(pitch > 0)
    def _():
        pitch_up().wait_recv()
        u = [halo[0, v] for v in range(n_var)]
        for v, value in enumerate(as_previous(u, flux_of(u, pressure_of(u), 2))):
            halo_in[0, v] = value

    @pl.when(pitch == 0)
    def _():
        for v in range(n_var):
            halo_in[0, v] = jnp.zeros((n_row, n_cell), jnp.float32)

    @pl.when(pitch < n_pitch - 1)
    def _():
        pitch_down().wait_recv()
        u = [halo[1, v] for v in range(n_var)]
        for v, value in enumerate(as_next(u, flux_of(u, pressure_of(u), 2))):
            halo_in[1, v] = value

    @pl.when(pitch == n_pitch - 1)
    def _():
        for v in range(n_var):
            halo_in[1, v] = jnp.zeros((n_row, n_cell), jnp.float32)

    span_copy.wait_recv()
    for side, form in enumerate((as_previous, as_next)):
        u = [span_rx[side]]
        for v in range(1, n_var):
            u.append(pltpu.roll(span_rx[side], LANES - v * n_row, 1))
        for v, value in enumerate(form(u, flux_of(u, pressure_of(u), 3))):
            span_in[side, v] = value

    load_step.wait()
    cell = lax.broadcasted_iota(jnp.int32, (n_col, n_cell), 1)
    col = lax.broadcasted_iota(jnp.int32, (n_col, n_cell), 0)

    def stencil(i, carry):
        before = [fx[v, i] for v in range(n_var)]
        after = [fx[v, i + 2] for v in range(n_var)]
        flux_before = flux_of(before, pressure_of(before), 1)
        flux_after = flux_of(after, pressure_of(after), 1)
        for v in range(n_var):
            out_v[v, i] = sx[v, i] + 0.125 * (before[v] + after[v]) + 0.25 * (flux_before[v] - flux_after[v])
        u = [fx[v, i + 1] for v in range(n_var)]
        p = pressure_of(u)
        flux = flux_of(u, p, 2)
        above = as_next(u, flux)
        below = as_previous(u, flux)
        for v in range(n_var):
            down = jnp.where(col == 0, halo_in[0, v, pl.ds(i, 1), :], pltpu.roll(below[v], 1, 0))
            up = jnp.where(col == n_col - 1, halo_in[1, v, pl.ds(i, 1), :], pltpu.roll(above[v], n_col - 1, 0))
            out_v[v, i] = out_v[v, i] + down + up - 0.75 * u[v]
        flux = flux_of(u, p, 3)
        above = as_next(u, flux)
        below = as_previous(u, flux)
        for v in range(n_var):
            first = pltpu.roll(span_in[0, v], LANES - i, 1)[:, :1]
            last = pltpu.roll(span_in[1, v], LANES - i, 1)[:, :1]
            down = jnp.where(cell == 0, first, pltpu.roll(below[v], 1, 1))
            up = jnp.where(cell == n_cell - 1, last, pltpu.roll(above[v], n_cell - 1, 1))
            out_v[v, i] = out_v[v, i] + down + up
        return carry

    lax.fori_loop(0, n_row, stencil, 0)
    store = pltpu.make_async_copy(out_v, acc_out, store_sem)
    store.start()

    @pl.when(is_end)
    def _():
        blade = is_blade(at)

        @pl.when(jnp.logical_not(blade))
        def _():
            pltpu.make_async_copy(
                slots.at[pl.ds(0, n_axial - 1)], recv.at[pl.ds(0, n_axial - 1)], row_recv).wait()

        @pl.when(blade & (span == n_span - 1))
        def _():
            pltpu.make_async_copy(
                slots.at[pl.ds(0, n_axial - 1), :, :, pl.ds(tail, LANES)],
                recv.at[pl.ds(0, n_axial - 1), :, :, pl.ds(tail, LANES)], row_recv).wait()

        position = lax.broadcasted_iota(jnp.int32, (1, n_cell), 1) + span * n_cell

        @pl.loop(0, n_row)
        def _(i):
            source = lax.div(partner[core, i], n_row)
            is_open = position >= n_span * n_cell - periodic[core, i]
            for v in range(n_var):
                wall = edge[core, v, pl.ds(i, 1), :]
                if v == 2:
                    wall = -wall
                ghost[v, pl.ds(i, 1), :] = jnp.where(is_open, recv[source, v], wall)

        u = [ghost[v] for v in range(n_var)]
        flux = flux_of(u, pressure_of(u), 2)
        sign = jnp.where(core == 0, 0.25, -0.25)
        for v in range(n_var):
            delta[v] = 0.125 * u[v] + sign * flux[v]

    @pl.when(jnp.logical_not(is_end))
    def _():
        for v in range(n_var):
            delta[v] = jnp.zeros((n_row, n_cell), jnp.float32)

    store_delta = pltpu.make_async_copy(delta, delta_out, delta_sem)
    store_delta.start()

    for v in range(n_var):
        core_copy(v).wait_send()

    @pl.when(jnp.logical_not(is_end))
    def _():
        for v in range(n_var):
            chain_copy(v).wait_send()

    @pl.when(is_end)
    def _():
        @pl.loop(1, n_axial)
        def _(j):
            target = lax.rem(at + j, n_axial)

            @pl.when(jnp.logical_not(is_blade(target)))
            def _():
                row_copy(target).wait_send()

            @pl.when(is_blade(target) & (span == n_span - 1))
            def _():
                tip_copy(target).wait_send()

    @pl.when(at < n_axial - 1)
    def _():
        axial_up().wait_send()

    @pl.when(at > 0)
    def _():
        axial_down().wait_send()

    @pl.when(pitch < n_pitch - 1)
    def _():
        pitch_up().wait_send()

    @pl.when(pitch > 0)
    def _():
        pitch_down().wait_send()

    span_copy.wait_send()
    store.wait()
    store_delta.wait()


def term_basis(phase_value, term_ids):
    harmonic = ((term_ids + 1) // 2).astype(phase_value.dtype)
    return jnp.where(
        (term_ids % 2 == 0) & (term_ids > 0), jnp.sin(harmonic * phase_value), jnp.cos(harmonic * phase_value))


def per_device(flow, step, lower_coef, upper_coef, partner, periodic, phase_angles):
    n_axial = lax.axis_size("axial")
    n_pitch = lax.axis_size("pitch")
    n_span = lax.axis_size("span")
    n_var, n_row, n_col, n_cell = flow.shape
    n_term = lower_coef.shape[0]
    pitch = lax.axis_index("pitch")
    term_ids = pitch * n_term + jnp.arange(n_term, dtype=jnp.int32)
    basis = term_basis(phase_angles[:, None], term_ids[None, :])
    sizes = (n_axial, n_pitch, n_span, n_var, n_row, n_col, n_cell, n_term)
    any_spec = pl.BlockSpec(memory_space=pl.ANY)
    smem = pl.BlockSpec(memory_space=pltpu.SMEM)
    face = (n_var, n_row, n_cell)
    f32 = jnp.float32
    dma = pltpu.SemaphoreType.DMA
    acc, delta = pl.pallas_call(
        functools.partial(kernel, sizes),
        out_shape=(jax.ShapeDtypeStruct(flow.shape, f32), jax.ShapeDtypeStruct(face, f32)),
        in_specs=[any_spec] * 4 + [smem] * 3,
        out_specs=(any_spec, any_spec),
        scratch_shapes=[
            pltpu.VMEM((n_var, n_row + 2, n_col, n_cell), f32),
            pltpu.VMEM(flow.shape, f32),
            pltpu.VMEM((2, n_term, *face), f32),
            pltpu.VMEM((2, *face), f32),
            pltpu.VMEM(face, f32),
            pltpu.VMEM(face, f32),
            pltpu.VMEM(face, f32),
            pltpu.VMEM((n_axial, n_var, 1, n_cell), f32),
            pltpu.VMEM((n_axial, n_var, 1, n_cell), f32),
            pltpu.VMEM((2, *face), f32),
            pltpu.VMEM((2, *face), f32),
            pltpu.VMEM((2, *face), f32),
            pltpu.VMEM((2, n_col, LANES), f32),
            pltpu.VMEM((2, n_col, LANES), f32),
            pltpu.VMEM((2, n_var, n_col, LANES), f32),
            pltpu.VMEM(flow.shape, f32),
            pltpu.VMEM(face, f32),
            pltpu.VMEM(face, f32),
            pltpu.SMEM((n_axial,), jnp.int32),
            dma((4,)), dma((n_var,)), dma((n_var,)), dma((n_var,)), dma((n_var,)), dma, dma,
            dma((2,)), dma((2,)), dma((2,)), dma((2,)), dma, dma, dma, dma,
        ],
        compiler_params=pltpu.CompilerParams(collective_id=0, has_side_effects=True),
        name="section",
    )(flow, step, lower_coef, upper_coef, basis, partner, periodic)
    edge_col = jnp.where(pitch == 0, 0, n_col - 1)
    col = lax.broadcasted_iota(jnp.int32, (1, 1, n_col, 1), 2)
    return acc + jnp.where(col == edge_col, delta[:, :, None, :], 0.0)


def solution(mesh):
    in_specs = (
        P(None, "axial", "pitch", "span"),
        P(None, "axial", "pitch", "span"),
        P("pitch", None, "axial", "span"),
        P("pitch", None, "axial", "span"),
        P(None, "axial"),
        P(None, "axial"),
        P(),
    )
    out_specs = P(None, "axial", "pitch", "span")
    return jax.shard_map(
        per_device, mesh=mesh, in_specs=in_specs, out_specs=out_specs, check_vma=False
    )
```

```python
import functools

import jax
import jax.numpy as jnp
from jax import lax
from jax.experimental import pallas as pl
from jax.experimental.pallas import tpu as pltpu
from jax.sharding import PartitionSpec as P

MESH = pl.DeviceIdType.MESH
LANES = 128


def pressure_of(u):
    kinetic = 0.5 * (u[1] * u[1] + u[2] * u[2] + u[3] * u[3]) / u[0]
    return 0.4 * (u[4] - kinetic)


def flux_of(u, pressure, direction):
    velocity = u[direction] / u[0]
    parts = [u[direction], u[1] * velocity, u[2] * velocity, u[3] * velocity, (u[4] + pressure) * velocity]
    parts[direction] = parts[direction] + pressure
    return parts


def as_previous(u, flux):
    return [0.125 * a + 0.25 * f for a, f in zip(u, flux)]


def as_next(u, flux):
    return [0.125 * a - 0.25 * f for a, f in zip(u, flux)]


def kernel(
    sizes, flow, step, lower_coef, upper_coef, phases, partner, periodic, out_v, sides,
    fx, sx, coef, part, rx_core, rx_near, rx_far, total, slots, recv, edge, halo, span_tx, span_rx, span_in,
    ghost, table,
    load_sem, core_send, core_recv, near_send, near_recv, far_send, far_recv, row_send, row_recv,
    axial_send, axial_recv, pitch_send, pitch_recv, span_send, span_recv, ready,
):
    n_axial, n_pitch, n_span, n_var, n_row, n_col, n_cell, n_term = sizes
    at = lax.axis_index("axial")
    pitch = lax.axis_index("pitch")
    span = lax.axis_index("span")
    chips = n_pitch // 2
    core = lax.rem(pitch, 2)
    chip = lax.div(pitch, 2)
    place = jnp.where(core == 0, chips - 1 - chip, chip)
    toward = 1 - 2 * core
    is_end = place == chips - 1
    is_helper = place == chips - 2
    is_middle = place == chips - 3
    is_start = place == chips - 4
    end = jnp.where(core == 0, 0, n_pitch - 1)
    helper = end + 2 * toward
    middle = end + 4 * toward
    mate = pitch + 1 - 2 * core
    beside = pitch - 1 + 2 * core
    has_beside = (beside >= 0) & (beside < n_pitch)
    tail = n_cell - LANES
    first_blade, end_blade = n_axial // 4, 3 * n_axial // 4

    def is_blade(a):
        return (a >= first_blade) & (a < end_blade)

    def load_coef(face):
        return [
            pltpu.make_async_copy(upper_coef, coef.at[0], load_sem.at[0]),
            pltpu.make_async_copy(lower_coef, coef.at[1], load_sem.at[1]),
        ][face]

    load_flow = pltpu.make_async_copy(flow, fx.at[:, pl.ds(1, n_row)], load_sem.at[2])
    load_step = pltpu.make_async_copy(step, sx, load_sem.at[3])
    @pl.when(core == 0)
    def _():
        load_coef(1).start()
        load_coef(0).start()

    @pl.when(core == 1)
    def _():
        load_coef(0).start()
        load_coef(1).start()

    load_flow.start()
    load_step.start()

    barrier = pltpu.get_barrier_semaphore()

    def greet(**where):
        pl.semaphore_signal(barrier, inc=1, device_id=where, device_id_type=MESH)

    one = jnp.int32(1)
    zero = jnp.int32(0)

    @pl.when(is_end)
    def _():
        @pl.loop(1, n_axial)
        def _(j):
            greet(axial=lax.rem(at + j, n_axial), pitch=helper)

    greetings = jnp.where(is_helper, n_axial - 1, 0)
    for holds, where in (
        (None, {"pitch": mate}),
        (None, {"span": 1 - span}),
        (has_beside, {"pitch": beside}),
        (pitch >= 2, {"pitch": pitch - 2}),
        (pitch < n_pitch - 2, {"pitch": pitch + 2}),
        (is_middle, {"pitch": end}),
        (is_end, {"pitch": middle}),
        (at > 0, {"axial": at - 1}),
        (at < n_axial - 1, {"axial": at + 1}),
    ):
        if holds is None:
            greet(**where)
            greetings = greetings + 1
        else:
            pl.when(holds)(functools.partial(greet, **where))
            greetings = greetings + jnp.where(holds, one, zero)

    spot = lax.broadcasted_iota(jnp.int32, (8, LANES), 1)
    second = spot >= n_term
    term = pitch * n_term + jnp.where(second, spot - n_term, spot)
    angle = lax.shift_right_logical(term + 1, 1).astype(jnp.float32) * jnp.where(second, phases[1], phases[0])
    basis = jnp.where((lax.rem(term, 2) == 0) & (term > 0), jnp.sin(angle), jnp.cos(angle))

    def evaluate(face, v):
        first = jnp.where(face == 0, basis, pltpu.roll(basis, LANES - n_term, 1))
        value = first[:1, :1] * coef[face, 0, v]
        for t in range(1, n_term):
            value = value + first[:1, t : t + 1] * coef[face, t, v]
        part[face, v] = value

    load_coef(0).wait()
    load_coef(1).wait()
    for v in range(n_var):
        evaluate(1 - core, v)

    pl.semaphore_wait(barrier, greetings)

    def core_copy(v):
        return pltpu.make_async_remote_copy(
            src_ref=part.at[1 - core, v], dst_ref=rx_core.at[v], send_sem=core_send.at[v], recv_sem=core_recv.at[v],
            device_id={"pitch": mate}, device_id_type=MESH)

    for v in range(n_var):
        core_copy(v).start()

    @pl.when(is_helper)
    def _():
        pl.semaphore_signal(ready, inc=1, device_id={"pitch": end}, device_id_type=MESH)

    for v in range(n_var):
        evaluate(core, v)

    load_flow.wait()

    def axial_up():
        return pltpu.make_async_remote_copy(
            src_ref=fx.at[:, n_row], dst_ref=fx.at[:, 0], send_sem=axial_send.at[0], recv_sem=axial_recv.at[0],
            device_id={"axial": at + 1}, device_id_type=MESH)

    def axial_down():
        return pltpu.make_async_remote_copy(
            src_ref=fx.at[:, 1], dst_ref=fx.at[:, n_row + 1], send_sem=axial_send.at[1], recv_sem=axial_recv.at[1],
            device_id={"axial": at - 1}, device_id_type=MESH)

    @pl.when(at < n_axial - 1)
    def _():
        axial_up().start()

    @pl.when(at > 0)
    def _():
        axial_down().start()

    lane = lax.broadcasted_iota(jnp.int32, (n_col, LANES), 1)
    span_copy = pltpu.make_async_remote_copy(
        src_ref=span_tx, dst_ref=span_rx, send_sem=span_send, recv_sem=span_recv,
        device_id={"span": 1 - span}, device_id_type=MESH)

    def pitch_up():
        return pltpu.make_async_remote_copy(
            src_ref=edge.at[1], dst_ref=halo.at[0], send_sem=pitch_send.at[0], recv_sem=pitch_recv.at[0],
            device_id={"pitch": pitch + 1}, device_id_type=MESH)

    def pitch_down():
        return pltpu.make_async_remote_copy(
            src_ref=edge.at[0], dst_ref=halo.at[1], send_sem=pitch_send.at[1], recv_sem=pitch_recv.at[1],
            device_id={"pitch": pitch - 1}, device_id_type=MESH)

    def pack(i, carry):
        low, high = carry
        for v in range(n_var):
            spot = v * n_row + i
            last = pltpu.roll(fx[v, i + 1, :, pl.ds(tail, LANES)], spot + 1, 1)
            first = pltpu.roll(fx[v, i + 1, :, pl.ds(0, LANES)], spot, 1)
            low = jnp.where(lane == spot, last, low)
            high = jnp.where(lane == spot, first, high)
            edge[0, v, pl.ds(i, 1), :] = fx[v, i + 1, pl.ds(0, 1), :]
            edge[1, v, pl.ds(i, 1), :] = fx[v, i + 1, pl.ds(n_col - 1, 1), :]
        return low, high

    def send_edges():
        blank = jnp.ones((n_col, LANES), jnp.float32)
        low, high = lax.fori_loop(0, n_row, pack, (blank, blank))
        span_tx[0] = low
        span_tx[1] = high
        span_copy.start()
        pl.when(core == 0)(lambda: pitch_up().start())
        pl.when(core == 1)(lambda: pitch_down().start())
        pl.when((core == 0) & (pitch > 0))(lambda: pitch_down().start())
        pl.when((core == 1) & (pitch < n_pitch - 1))(lambda: pitch_up().start())

    early = is_end | is_middle
    pl.when(early)(send_edges)

    @pl.when(is_end)
    def _():
        @pl.loop(0, n_axial)
        def _(d):
            index = jnp.int32(0)
            for r in range(n_row):
                index = jnp.where(lax.div(partner[1 - core, r], n_row) == d, r, index)
            table[d] = index

    def near_copy(v):
        return pltpu.make_async_remote_copy(
            src_ref=total.at[v], dst_ref=rx_near.at[v], send_sem=near_send.at[v], recv_sem=near_recv.at[v],
            device_id={"pitch": pitch - 2 * toward}, device_id_type=MESH)

    def far_copy(v):
        return pltpu.make_async_remote_copy(
            src_ref=total.at[v], dst_ref=rx_far.at[v], send_sem=far_send.at[v], recv_sem=far_recv.at[v],
            device_id={"pitch": end}, device_id_type=MESH)

    for v in range(n_var):
        core_copy(v).wait_recv()
        total[v] = part[core, v] + rx_core[v]
        pl.when(is_start | is_helper)(lambda: near_copy(v).start())

    pl.when(jnp.logical_not(early))(send_edges)

    if chips > 2:
        @pl.when(is_middle)
        def _():
            for v in range(n_var):
                if chips > 3:
                    near_copy(v).wait_recv()
                    total[v] = total[v] + rx_near[v]
                far_copy(v).start()

    def row_copy(target):
        return pltpu.make_async_remote_copy(
            src_ref=slots.at[target], dst_ref=recv.at[at], send_sem=row_send, recv_sem=row_recv,
            device_id={"axial": target}, device_id_type=MESH)

    def tip_copy(target):
        return pltpu.make_async_remote_copy(
            src_ref=slots.at[target, :, :, pl.ds(tail, LANES)], dst_ref=recv.at[at, :, :, pl.ds(tail, LANES)],
            send_sem=row_send, recv_sem=row_recv, device_id={"axial": target}, device_id_type=MESH)

    @pl.when(is_end)
    def _():
        for v in range(n_var):
            near_copy(v).wait_recv()
            total[v] = total[v] + rx_near[v]
            if chips > 2:
                far_copy(v).wait_recv()
                total[v] = total[v] + rx_far[v]

            @pl.loop(0, n_axial)
            def _(d):
                slots[d, v] = total[v, pl.ds(table[d], 1), :]

        pl.semaphore_wait(ready, 1)

        @pl.loop(1, n_axial)
        def _(j):
            target = lax.rem(at + j, n_axial)
            pl.when(jnp.logical_not(is_blade(target)))(lambda: row_copy(target).start())
            pl.when(is_blade(target) & (span == n_span - 1))(lambda: tip_copy(target).start())

        own = table[at]
        for v in range(n_var):
            recv[at, v] = total[v, pl.ds(own, 1), :]

    span_copy.wait_recv()

    @pl.when(at > 0)
    def _():
        axial_up().wait_recv()

    @pl.when(at == 0)
    def _():
        for v in range(n_var):
            fx[v, 0] = fx[v, 1]

    @pl.when(at < n_axial - 1)
    def _():
        axial_down().wait_recv()

    @pl.when(at == n_axial - 1)
    def _():
        for v in range(n_var):
            fx[v, n_row + 1] = fx[v, n_row]

    for side, form in enumerate((as_previous, as_next)):
        u = [span_rx[side]]
        for v in range(1, n_var):
            u.append(pltpu.roll(span_rx[side], LANES - v * n_row, 1))
        for v, value in enumerate(form(u, flux_of(u, pressure_of(u), 3))):
            span_in[side, v] = value

    load_step.wait()
    cell = lax.broadcasted_iota(jnp.int32, (n_col, n_cell), 1)
    col = lax.broadcasted_iota(jnp.int32, (n_col, n_cell), 0)

    def stencil(i, carry):
        before = [fx[v, i] for v in range(n_var)]
        after = [fx[v, i + 2] for v in range(n_var)]
        flux_before = flux_of(before, pressure_of(before), 1)
        flux_after = flux_of(after, pressure_of(after), 1)
        for v in range(n_var):
            out_v[v, i] = sx[v, i] + 0.125 * (before[v] + after[v]) + 0.25 * (flux_before[v] - flux_after[v])
        u = [fx[v, i + 1] for v in range(n_var)]
        p = pressure_of(u)
        flux = flux_of(u, p, 2)
        above = as_next(u, flux)
        below = as_previous(u, flux)
        for v in range(n_var):
            down = jnp.where(col == 0, 0.0, pltpu.roll(below[v], 1, 0))
            up = jnp.where(col == n_col - 1, 0.0, pltpu.roll(above[v], n_col - 1, 0))
            out_v[v, i] = out_v[v, i] + down + up - 0.75 * u[v]
        flux = flux_of(u, p, 3)
        above = as_next(u, flux)
        below = as_previous(u, flux)
        for v in range(n_var):
            first = pltpu.roll(span_in[0, v], LANES - i, 1)[:, :1]
            last = pltpu.roll(span_in[1, v], LANES - i, 1)[:, :1]
            down = jnp.where(cell == 0, first, pltpu.roll(below[v], 1, 1))
            up = jnp.where(cell == n_cell - 1, last, pltpu.roll(above[v], n_cell - 1, 1))
            out_v[v, i] = out_v[v, i] + down + up
        return carry

    lax.fori_loop(0, n_row, stencil, 0)

    def add_side(side, u):
        form = (as_previous, as_next)[side]
        for v, value in enumerate(form(u, flux_of(u, pressure_of(u), 2))):
            sides[side, v] = value

    @pl.when(pitch > 0)
    def _():
        pitch_up().wait_recv()
        add_side(0, [halo[0, v] for v in range(n_var)])

    @pl.when(pitch < n_pitch - 1)
    def _():
        pitch_down().wait_recv()
        add_side(1, [halo[1, v] for v in range(n_var)])

    @pl.when(is_end)
    def _():
        blade = is_blade(at)

        @pl.when(jnp.logical_not(blade))
        def _():
            pltpu.make_async_copy(
                slots.at[pl.ds(0, n_axial - 1)], recv.at[pl.ds(0, n_axial - 1)], row_recv).wait()

        @pl.when(blade & (span == n_span - 1))
        def _():
            pltpu.make_async_copy(
                slots.at[pl.ds(0, n_axial - 1), :, :, pl.ds(tail, LANES)],
                recv.at[pl.ds(0, n_axial - 1), :, :, pl.ds(tail, LANES)], row_recv).wait()

        position = lax.broadcasted_iota(jnp.int32, (1, n_cell), 1) + span * n_cell

        @pl.loop(0, n_row)
        def _(i):
            source = lax.div(partner[core, i], n_row)
            is_open = position >= n_span * n_cell - periodic[core, i]
            for v in range(n_var):
                wall = edge[core, v, pl.ds(i, 1), :]
                if v == 2:
                    wall = -wall
                ghost[v, pl.ds(i, 1), :] = jnp.where(is_open, recv[source, v], wall)

        pl.when(core == 0)(lambda: add_side(0, [ghost[v] for v in range(n_var)]))
        pl.when(core == 1)(lambda: add_side(1, [ghost[v] for v in range(n_var)]))

    for v in range(n_var):
        core_copy(v).wait_send()

    @pl.when(is_start | is_helper)
    def _():
        for v in range(n_var):
            near_copy(v).wait_send()

    if chips > 2:
        @pl.when(is_middle)
        def _():
            for v in range(n_var):
                far_copy(v).wait_send()

    @pl.when(is_end)
    def _():
        @pl.loop(1, n_axial)
        def _(j):
            target = lax.rem(at + j, n_axial)

            @pl.when(jnp.logical_not(is_blade(target)))
            def _():
                row_copy(target).wait_send()

            @pl.when(is_blade(target) & (span == n_span - 1))
            def _():
                tip_copy(target).wait_send()

    @pl.when(at < n_axial - 1)
    def _():
        axial_up().wait_send()

    @pl.when(at > 0)
    def _():
        axial_down().wait_send()

    @pl.when(pitch < n_pitch - 1)
    def _():
        pitch_up().wait_send()

    @pl.when(pitch > 0)
    def _():
        pitch_down().wait_send()

    span_copy.wait_send()


def per_device(flow, step, lower_coef, upper_coef, partner, periodic, phase_angles):
    n_axial = lax.axis_size("axial")
    n_pitch = lax.axis_size("pitch")
    n_span = lax.axis_size("span")
    n_var, n_row, n_col, n_cell = flow.shape
    n_term = lower_coef.shape[0]
    sizes = (n_axial, n_pitch, n_span, n_var, n_row, n_col, n_cell, n_term)
    any_spec = pl.BlockSpec(memory_space=pl.ANY)
    vmem = pl.BlockSpec(memory_space=pltpu.VMEM)
    smem = pl.BlockSpec(memory_space=pltpu.SMEM)
    face = (n_var, n_row, n_cell)
    f32 = jnp.float32
    dma = pltpu.SemaphoreType.DMA
    flow, step, lower_coef, upper_coef, phase_angles, partner, periodic = (
        pltpu.with_memory_space_constraint(a, pltpu.HBM)
        for a in (flow, step, lower_coef, upper_coef, phase_angles, partner, periodic))
    acc, sides = pl.pallas_call(
        functools.partial(kernel, sizes),
        out_shape=(pltpu.VMEM(flow.shape, f32), pltpu.VMEM((2, *face), f32)),
        in_specs=[any_spec] * 4 + [smem] * 3,
        out_specs=(vmem, vmem),
        scratch_shapes=[
            pltpu.VMEM((n_var, n_row + 2, n_col, n_cell), f32),
            pltpu.VMEM(flow.shape, f32),
            pltpu.VMEM((2, n_term, *face), f32),
            pltpu.VMEM((2, *face), f32),
            pltpu.VMEM(face, f32),
            pltpu.VMEM(face, f32),
            pltpu.VMEM(face, f32),
            pltpu.VMEM(face, f32),
            pltpu.VMEM((n_axial, n_var, 1, n_cell), f32),
            pltpu.VMEM((n_axial, n_var, 1, n_cell), f32),
            pltpu.VMEM((2, *face), f32),
            pltpu.VMEM((2, *face), f32),
            pltpu.VMEM((2, n_col, LANES), f32),
            pltpu.VMEM((2, n_col, LANES), f32),
            pltpu.VMEM((2, n_var, n_col, LANES), f32),
            pltpu.VMEM(face, f32),
            pltpu.SMEM((n_axial,), jnp.int32),
            dma((4,)), dma((n_var,)), dma((n_var,)), dma((n_var,)), dma((n_var,)),
            dma((n_var,)), dma((n_var,)), dma, dma, dma((2,)), dma((2,)), dma((2,)), dma((2,)), dma, dma,
            pltpu.SemaphoreType.REGULAR,
        ],
        compiler_params=pltpu.CompilerParams(collective_id=0, has_side_effects=True, vmem_limit_bytes=24 << 20),
        name="section",
    )(flow, step, lower_coef, upper_coef, phase_angles, partner, periodic)
    col = lax.broadcasted_iota(jnp.int32, (1, 1, n_col, 1), 2)
    low, high = sides[0][:, :, None, :], sides[1][:, :, None, :]
    return acc + jnp.where(col == 0, low, jnp.where(col == n_col - 1, high, 0.0))


def solution(mesh):
    in_specs = (
        P(None, "axial", "pitch", "span"),
        P(None, "axial", "pitch", "span"),
        P("pitch", None, "axial", "span"),
        P("pitch", None, "axial", "span"),
        P(None, "axial"),
        P(None, "axial"),
        P(),
    )
    out_specs = P(None, "axial", "pitch", "span")
    return jax.shard_map(
        per_device, mesh=mesh, in_specs=in_specs, out_specs=out_specs, check_vma=False
    )
```

```python
import functools

import jax
import jax.numpy as jnp
from jax import lax
from jax.experimental import pallas as pl
from jax.experimental.pallas import tpu as pltpu
from jax.sharding import PartitionSpec as P

MESH = pl.DeviceIdType.MESH
LANES = 128


def pressure_of(u):
    kinetic = 0.5 * (u[1] * u[1] + u[2] * u[2] + u[3] * u[3]) / u[0]
    return 0.4 * (u[4] - kinetic)


def flux_of(u, pressure, direction):
    velocity = u[direction] / u[0]
    parts = [u[direction], u[1] * velocity, u[2] * velocity, u[3] * velocity, (u[4] + pressure) * velocity]
    parts[direction] = parts[direction] + pressure
    return parts


def as_previous(u, flux):
    return [0.125 * a + 0.25 * f for a, f in zip(u, flux)]


def as_next(u, flux):
    return [0.125 * a - 0.25 * f for a, f in zip(u, flux)]


def kernel(
    sizes, flow, step, lower_coef, upper_coef, phases_in, partner_in, periodic_in, out_v, sides,
    fx, sx, coef, part, rx_core, rx_near, rx_far, total, slots, recv, edge, halo, span_tx, span_rx, span_in,
    ghost, phases, partner, periodic, table,
    load_sem, core_send, core_recv, near_send, near_recv, far_send, far_recv, row_send, row_recv,
    axial_send, axial_recv, pitch_send, pitch_recv, span_send, span_recv, ready, span_ready,
):
    n_axial, n_pitch, n_span, n_var, n_row, n_col, n_cell, n_term = sizes
    at = lax.axis_index("axial")
    pitch = lax.axis_index("pitch")
    span = lax.axis_index("span")
    chips = n_pitch // 2
    n_z = min(n_axial, 8)
    core = lax.rem(pitch, 2)
    chip = lax.div(pitch, 2)
    place = jnp.where(core == 0, chips - 1 - chip, chip)
    toward = 1 - 2 * core
    is_end = place == chips - 1
    is_helper = place == chips - 2
    is_middle = place == chips - 3
    is_start = place == chips - 4
    end = jnp.where(core == 0, 0, n_pitch - 1)
    helper = end + 2 * toward
    middle = end + 4 * toward
    mate = pitch + 1 - 2 * core
    beside = pitch - 1 + 2 * core
    has_beside = (beside >= 0) & (beside < n_pitch)
    tail = n_cell - LANES
    first_blade, end_blade = n_axial // 4, 3 * n_axial // 4

    def is_blade(a):
        return (a >= first_blade) & (a < end_blade)

    def load_coef(face):
        return [
            pltpu.make_async_copy(upper_coef, coef.at[0], load_sem.at[0]),
            pltpu.make_async_copy(lower_coef, coef.at[1], load_sem.at[1]),
        ][face]

    load_flow = pltpu.make_async_copy(flow, fx.at[:, pl.ds(1, n_row)], load_sem.at[2])
    load_step = pltpu.make_async_copy(step, sx, load_sem.at[3])
    load_phases = pltpu.make_async_copy(phases_in, phases, load_sem.at[4])
    load_partner = pltpu.make_async_copy(partner_in, partner, load_sem.at[5])
    load_periodic = pltpu.make_async_copy(periodic_in, periodic, load_sem.at[6])
    load_phases.start()
    @pl.when(core == 0)
    def _():
        load_coef(1).start()
        load_coef(0).start()

    @pl.when(core == 1)
    def _():
        load_coef(0).start()
        load_coef(1).start()

    load_partner.start()
    load_periodic.start()

    barrier = pltpu.get_barrier_semaphore()

    def greet(**where):
        pl.semaphore_signal(barrier, inc=1, device_id=where, device_id_type=MESH)

    one = jnp.int32(1)
    zero = jnp.int32(0)

    def tell(sem, **where):
        pl.semaphore_signal(sem, inc=1, device_id=where, device_id_type=MESH)

    @pl.when(is_end)
    def _():
        @pl.loop(1, n_axial)
        def _(j):
            greet(axial=lax.rem(at + j, n_axial), pitch=helper)

    pl.when(is_end)(lambda: greet(pitch=helper))
    pl.when(is_end)(lambda: greet(pitch=middle))
    pl.when(is_middle)(lambda: greet(pitch=pitch + 2 * toward))
    greetings = jnp.where(is_helper, n_axial - 1, zero) + jnp.where(is_end, zero, one)
    greet(span=1 - span, pitch=jnp.where(span == 1, n_pitch - 3, 2))
    collector = jnp.where(span == 0, n_pitch - 3, 2)
    is_collector = pitch == collector
    pl.when(jnp.logical_not(is_collector))(lambda: greet(pitch=collector))
    greetings = greetings + jnp.where(is_collector, 2 * n_pitch - 1, zero)
    for holds, where in (
        (None, {"pitch": mate}),
        (has_beside, {"pitch": beside}),
        (at > 0, {"axial": at - 1}),
        (at < n_axial - 1, {"axial": at + 1}),
    ):
        if holds is None:
            greet(**where)
            greetings = greetings + 1
        else:
            pl.when(holds)(functools.partial(greet, **where))
            greetings = greetings + jnp.where(holds, one, zero)

    load_phases.wait()
    spot = lax.broadcasted_iota(jnp.int32, (8, LANES), 1)
    second = spot >= n_term
    term = pitch * n_term + jnp.where(second, spot - n_term, spot)
    angle = lax.shift_right_logical(term + 1, 1).astype(jnp.float32) * jnp.where(second, phases[1], phases[0])
    basis = jnp.where((lax.rem(term, 2) == 0) & (term > 0), jnp.sin(angle), jnp.cos(angle))

    def evaluate(face, v):
        first = jnp.where(face == 0, basis, pltpu.roll(basis, LANES - n_term, 1))
        value = first[:1, :1] * coef[face, 0, v]
        for t in range(1, n_term):
            value = value + first[:1, t : t + 1] * coef[face, t, v]
        part[face, v] = value

    pl.when(core == 0)(lambda: load_coef(1).wait())
    pl.when(core == 1)(lambda: load_coef(0).wait())
    load_flow.start()
    for v in range(n_var):
        evaluate(1 - core, v)

    pl.semaphore_wait(barrier, greetings)

    def core_copy(v):
        return pltpu.make_async_remote_copy(
            src_ref=part.at[1 - core, v], dst_ref=rx_core.at[v], send_sem=core_send.at[v], recv_sem=core_recv.at[v],
            device_id={"pitch": mate}, device_id_type=MESH)

    for v in range(n_var):
        core_copy(v).start()

    pl.when(is_helper)(lambda: tell(ready, pitch=end))

    @pl.when(is_collector)
    def _():
        for k in range(n_pitch):
            pl.when(pitch != k)(lambda: tell(span_ready, pitch=k))

    load_step.start()
    pl.when(core == 0)(lambda: load_coef(0).wait())
    pl.when(core == 1)(lambda: load_coef(1).wait())
    for v in range(n_var):
        evaluate(core, v)

    def near_copy(v):
        return pltpu.make_async_remote_copy(
            src_ref=total.at[v], dst_ref=rx_near.at[v], send_sem=near_send.at[v], recv_sem=near_recv.at[v],
            device_id={"pitch": pitch - 2 * toward}, device_id_type=MESH)

    def far_copy(v):
        return pltpu.make_async_remote_copy(
            src_ref=total.at[v], dst_ref=rx_far.at[v], send_sem=far_send.at[v], recv_sem=far_recv.at[v],
            device_id={"pitch": end}, device_id_type=MESH)

    for v in range(n_var):
        core_copy(v).wait_recv()
        total[v] = part[core, v] + rx_core[v]
        pl.when(is_start | is_helper)(lambda: near_copy(v).start())

    load_flow.wait()

    def axial_up():
        return pltpu.make_async_remote_copy(
            src_ref=fx.at[:, n_row], dst_ref=fx.at[:, 0], send_sem=axial_send.at[0], recv_sem=axial_recv.at[0],
            device_id={"axial": at + 1}, device_id_type=MESH)

    def axial_down():
        return pltpu.make_async_remote_copy(
            src_ref=fx.at[:, 1], dst_ref=fx.at[:, n_row + 1], send_sem=axial_send.at[1], recv_sem=axial_recv.at[1],
            device_id={"axial": at - 1}, device_id_type=MESH)

    @pl.when(at < n_axial - 1)
    def _():
        axial_up().start()

    @pl.when(at > 0)
    def _():
        axial_down().start()

    lane = lax.broadcasted_iota(jnp.int32, (n_col, LANES), 1)
    span_copy = pltpu.make_async_remote_copy(
        src_ref=span_tx, dst_ref=span_rx, send_sem=span_send, recv_sem=span_recv,
        device_id={"span": 1 - span}, device_id_type=MESH)

    def pitch_up():
        return pltpu.make_async_remote_copy(
            src_ref=edge.at[1], dst_ref=halo.at[0], send_sem=pitch_send.at[0], recv_sem=pitch_recv.at[0],
            device_id={"pitch": pitch + 1}, device_id_type=MESH)

    def pitch_down():
        return pltpu.make_async_remote_copy(
            src_ref=edge.at[0], dst_ref=halo.at[1], send_sem=pitch_send.at[1], recv_sem=pitch_recv.at[1],
            device_id={"pitch": pitch - 1}, device_id_type=MESH)

    def pack(i, carry):
        low, high = carry
        for v in range(n_var):
            spot = v * n_row + i
            last = pltpu.roll(fx[v, i + 1, :, pl.ds(tail, LANES)], spot + 1, 1)
            first = pltpu.roll(fx[v, i + 1, :, pl.ds(0, LANES)], spot, 1)
            low = jnp.where(lane == spot, last, low)
            high = jnp.where(lane == spot, first, high)
            edge[0, v, pl.ds(i, 1), :] = fx[v, i + 1, pl.ds(0, 1), :]
            edge[1, v, pl.ds(i, 1), :] = fx[v, i + 1, pl.ds(n_col - 1, 1), :]
        return low, high

    def send_edges():
        blank = jnp.ones((n_col, LANES), jnp.float32)
        low, high = lax.fori_loop(0, n_row, pack, (blank, blank))
        span_tx[0] = low
        span_tx[1] = high
        pl.when(core == 0)(lambda: pitch_up().start())
        pl.when(core == 1)(lambda: pitch_down().start())
        pl.when((core == 0) & (pitch > 0) & jnp.logical_not(is_middle))(lambda: pitch_down().start())
        pl.when((core == 1) & (pitch < n_pitch - 1) & jnp.logical_not(is_middle))(lambda: pitch_up().start())

    def send_span():
        pl.when(jnp.logical_not(is_collector))(lambda: pl.semaphore_wait(span_ready, 1))
        span_copy.start()

    send_edges()


    load_partner.wait()
    load_periodic.wait()

    @pl.when(is_end)
    def _():
        @pl.loop(0, n_axial)
        def _(d):
            index = jnp.int32(0)
            for r in range(n_row):
                index = jnp.where(lax.div(partner[1 - core, r], n_row) == d, r, index)
            table[d] = index

    if chips > 2:
        @pl.when(is_middle)
        def _():
            for v in range(n_var):
                if chips > 3:
                    near_copy(v).wait_recv()
                    total[v] = total[v] + rx_near[v]
                far_copy(v).start()
            pl.when(core == 0)(lambda: pitch_down().start())
            pl.when(core == 1)(lambda: pitch_up().start())

    send_span()

    def row_copy(target):
        return pltpu.make_async_remote_copy(
            src_ref=slots.at[target], dst_ref=recv.at[at], send_sem=row_send, recv_sem=row_recv,
            device_id={"axial": target}, device_id_type=MESH)

    def tip_copy(target):
        return pltpu.make_async_remote_copy(
            src_ref=slots.at[target, :, :, pl.ds(tail, LANES)], dst_ref=recv.at[at, :, :, pl.ds(tail, LANES)],
            send_sem=row_send, recv_sem=row_recv, device_id={"axial": target}, device_id_type=MESH)

    @pl.when(is_end)
    def _():
        for v in range(n_var):
            near_copy(v).wait_recv()
            total[v] = total[v] + rx_near[v]
            if chips > 2:
                far_copy(v).wait_recv()
                total[v] = total[v] + rx_far[v]

            @pl.loop(0, n_axial)
            def _(d):
                slots[d, v] = total[v, pl.ds(table[d], 1), :]

        pl.semaphore_wait(ready, 1)

        order = sorted(range(n_axial), key=lambda d: (first_blade <= d < end_blade, d % n_z))
        for target in order:
            if first_blade <= target < end_blade:
                pl.when((at != target) & (span == n_span - 1))(lambda: tip_copy(target).start())
            else:
                pl.when(at != target)(lambda: row_copy(target).start())

        own = table[at]
        for v in range(n_var):
            recv[at, v] = total[v, pl.ds(own, 1), :]

    load_step.wait()
    cell = lax.broadcasted_iota(jnp.int32, (n_col, n_cell), 1)
    col = lax.broadcasted_iota(jnp.int32, (n_col, n_cell), 0)

    def stencil(i, carry):
        before = [fx[v, i] for v in range(n_var)]
        after = [fx[v, i + 2] for v in range(n_var)]
        flux_before = flux_of(before, pressure_of(before), 1)
        flux_after = flux_of(after, pressure_of(after), 1)
        for v in range(n_var):
            out_v[v, i] = sx[v, i] + 0.125 * (before[v] + after[v]) + 0.25 * (flux_before[v] - flux_after[v])
        u = [fx[v, i + 1] for v in range(n_var)]
        p = pressure_of(u)
        flux = flux_of(u, p, 2)
        above = as_next(u, flux)
        below = as_previous(u, flux)
        for v in range(n_var):
            down = jnp.where(col == 0, 0.0, pltpu.roll(below[v], 1, 0))
            up = jnp.where(col == n_col - 1, 0.0, pltpu.roll(above[v], n_col - 1, 0))
            out_v[v, i] = out_v[v, i] + down + up - 0.75 * u[v]
        flux = flux_of(u, p, 3)
        above = as_next(u, flux)
        below = as_previous(u, flux)
        for v in range(n_var):
            down = jnp.where(cell == 0, 0.0, pltpu.roll(below[v], 1, 1))
            up = jnp.where(cell == n_cell - 1, 0.0, pltpu.roll(above[v], n_cell - 1, 1))
            out_v[v, i] = out_v[v, i] + down + up
        return carry

    lax.fori_loop(1, n_row - 1, stencil, 0)


    @pl.when(at > 0)
    def _():
        axial_up().wait_recv()

    @pl.when(at == 0)
    def _():
        for v in range(n_var):
            fx[v, 0] = fx[v, 1]

    @pl.when(at < n_axial - 1)
    def _():
        axial_down().wait_recv()

    @pl.when(at == n_axial - 1)
    def _():
        for v in range(n_var):
            fx[v, n_row + 1] = fx[v, n_row]

    lax.fori_loop(0, 2, lambda k, carry: stencil(k * (n_row - 1), carry), 0)

    span_copy.wait_recv()
    for side, form in enumerate((as_previous, as_next)):
        u = [span_rx[side]]
        for v in range(1, n_var):
            u.append(pltpu.roll(span_rx[side], LANES - v * n_row, 1))
        for v, value in enumerate(form(u, flux_of(u, pressure_of(u), 3))):
            span_in[side, v] = value

    def add_span(i, carry):
        for v in range(n_var):
            first = jnp.where(lane == 0, pltpu.roll(span_in[0, v], LANES - i, 1), 0.0)
            last = jnp.where(lane == LANES - 1, pltpu.roll(span_in[1, v], LANES - 1 - i, 1), 0.0)
            out_v[v, i, :, pl.ds(0, LANES)] = out_v[v, i, :, pl.ds(0, LANES)] + first
            out_v[v, i, :, pl.ds(tail, LANES)] = out_v[v, i, :, pl.ds(tail, LANES)] + last
        return carry

    lax.fori_loop(0, n_row, add_span, 0)


    def add_side(side, u):
        form = (as_previous, as_next)[side]
        for v, value in enumerate(form(u, flux_of(u, pressure_of(u), 2))):
            sides[side, v] = value

    @pl.when(pitch > 0)
    def _():
        pitch_up().wait_recv()
        add_side(0, [halo[0, v] for v in range(n_var)])

    @pl.when(pitch < n_pitch - 1)
    def _():
        pitch_down().wait_recv()
        add_side(1, [halo[1, v] for v in range(n_var)])

    @pl.when(is_end)
    def _():
        blade = is_blade(at)

        @pl.when(jnp.logical_not(blade))
        def _():
            pltpu.make_async_copy(
                slots.at[pl.ds(0, n_axial - 1)], recv.at[pl.ds(0, n_axial - 1)], row_recv).wait()

        @pl.when(blade & (span == n_span - 1))
        def _():
            pltpu.make_async_copy(
                slots.at[pl.ds(0, n_axial - 1), :, :, pl.ds(tail, LANES)],
                recv.at[pl.ds(0, n_axial - 1), :, :, pl.ds(tail, LANES)], row_recv).wait()

        position = lax.broadcasted_iota(jnp.int32, (1, n_cell), 1) + span * n_cell

        @pl.loop(0, n_row)
        def _(i):
            source = lax.div(partner[core, i], n_row)
            is_open = position >= n_span * n_cell - periodic[core, i]
            for v in range(n_var):
                wall = edge[core, v, pl.ds(i, 1), :]
                if v == 2:
                    wall = -wall
                ghost[v, pl.ds(i, 1), :] = jnp.where(is_open, recv[source, v], wall)

        pl.when(core == 0)(lambda: add_side(0, [ghost[v] for v in range(n_var)]))
        pl.when(core == 1)(lambda: add_side(1, [ghost[v] for v in range(n_var)]))

    for v in range(n_var):
        core_copy(v).wait_send()

    @pl.when(is_start | is_helper)
    def _():
        for v in range(n_var):
            near_copy(v).wait_send()

    if chips > 2:
        @pl.when(is_middle)
        def _():
            for v in range(n_var):
                far_copy(v).wait_send()

    @pl.when(is_end)
    def _():
        @pl.loop(1, n_axial)
        def _(j):
            target = lax.rem(at + j, n_axial)

            @pl.when(jnp.logical_not(is_blade(target)))
            def _():
                row_copy(target).wait_send()

            @pl.when(is_blade(target) & (span == n_span - 1))
            def _():
                tip_copy(target).wait_send()

    @pl.when(at < n_axial - 1)
    def _():
        axial_up().wait_send()

    @pl.when(at > 0)
    def _():
        axial_down().wait_send()

    @pl.when(pitch < n_pitch - 1)
    def _():
        pitch_up().wait_send()

    @pl.when(pitch > 0)
    def _():
        pitch_down().wait_send()

    span_copy.wait_send()


def per_device(flow, step, lower_coef, upper_coef, partner, periodic, phase_angles):
    n_axial = lax.axis_size("axial")
    n_pitch = lax.axis_size("pitch")
    n_span = lax.axis_size("span")
    n_var, n_row, n_col, n_cell = flow.shape
    n_term = lower_coef.shape[0]
    sizes = (n_axial, n_pitch, n_span, n_var, n_row, n_col, n_cell, n_term)
    any_spec = pl.BlockSpec(memory_space=pl.ANY)
    vmem = pl.BlockSpec(memory_space=pltpu.VMEM)
    face = (n_var, n_row, n_cell)
    f32 = jnp.float32
    dma = pltpu.SemaphoreType.DMA
    flow, step, lower_coef, upper_coef, phase_angles, partner, periodic = (
        pltpu.with_memory_space_constraint(a, pltpu.HBM)
        for a in (flow, step, lower_coef, upper_coef, phase_angles, partner, periodic))
    acc, sides = pl.pallas_call(
        functools.partial(kernel, sizes),
        out_shape=(pltpu.VMEM(flow.shape, f32), pltpu.VMEM((2, *face), f32)),
        in_specs=[any_spec] * 7,
        out_specs=(vmem, vmem),
        scratch_shapes=[
            pltpu.VMEM((n_var, n_row + 2, n_col, n_cell), f32),
            pltpu.VMEM(flow.shape, f32),
            pltpu.VMEM((2, n_term, *face), f32),
            pltpu.VMEM((2, *face), f32),
            pltpu.VMEM(face, f32),
            pltpu.VMEM(face, f32),
            pltpu.VMEM(face, f32),
            pltpu.VMEM(face, f32),
            pltpu.VMEM((n_axial, n_var, 1, n_cell), f32),
            pltpu.VMEM((n_axial, n_var, 1, n_cell), f32),
            pltpu.VMEM((2, *face), f32),
            pltpu.VMEM((2, *face), f32),
            pltpu.VMEM((2, n_col, LANES), f32),
            pltpu.VMEM((2, n_col, LANES), f32),
            pltpu.VMEM((2, n_var, n_col, LANES), f32),
            pltpu.VMEM(face, f32),
            pltpu.SMEM(phase_angles.shape, f32),
            pltpu.SMEM(partner.shape, jnp.int32),
            pltpu.SMEM(periodic.shape, jnp.int32),
            pltpu.SMEM((n_axial,), jnp.int32),
            dma((7,)), dma((n_var,)), dma((n_var,)), dma((n_var,)), dma((n_var,)),
            dma((n_var,)), dma((n_var,)), dma, dma, dma((2,)), dma((2,)), dma((2,)), dma((2,)), dma, dma,
            pltpu.SemaphoreType.REGULAR, pltpu.SemaphoreType.REGULAR,
        ],
        compiler_params=pltpu.CompilerParams(collective_id=0, has_side_effects=True, vmem_limit_bytes=24 << 20),
        name="section",
    )(flow, step, lower_coef, upper_coef, phase_angles, partner, periodic)
    col = lax.broadcasted_iota(jnp.int32, (1, 1, n_col, 1), 2)
    low, high = sides[0][:, :, None, :], sides[1][:, :, None, :]
    return acc + jnp.where(col == 0, low, jnp.where(col == n_col - 1, high, 0.0))


def solution(mesh):
    in_specs = (
        P(None, "axial", "pitch", "span"),
        P(None, "axial", "pitch", "span"),
        P("pitch", None, "axial", "span"),
        P("pitch", None, "axial", "span"),
        P(None, "axial"),
        P(None, "axial"),
        P(),
    )
    out_specs = P(None, "axial", "pitch", "span")
    return jax.shard_map(
        per_device, mesh=mesh, in_specs=in_specs, out_specs=out_specs, check_vma=False
    )
```

```python
import functools

import jax
import jax.numpy as jnp
from jax import lax
from jax.experimental import pallas as pl
from jax.experimental.pallas import tpu as pltpu
from jax.sharding import PartitionSpec as P

MESH = pl.DeviceIdType.MESH
LANES = 128


def pressure_of(u):
    kinetic = 0.5 * (u[1] * u[1] + u[2] * u[2] + u[3] * u[3]) / u[0]
    return 0.4 * (u[4] - kinetic)


def flux_of(u, pressure, direction):
    velocity = u[direction] / u[0]
    parts = [u[direction], u[1] * velocity, u[2] * velocity, u[3] * velocity, (u[4] + pressure) * velocity]
    parts[direction] = parts[direction] + pressure
    return parts


def as_previous(u, flux):
    return [0.125 * a + 0.25 * f for a, f in zip(u, flux)]


def as_next(u, flux):
    return [0.125 * a - 0.25 * f for a, f in zip(u, flux)]


def kernel(
    sizes, flow, step, lower_coef, upper_coef, phases_in, partner_in, periodic_in, out_v, sides,
    fx, sx, coef, part, rx_core, rx_near, rx_far, total, slots, recv, edge, halo, span_tx, span_rx, span_in,
    ghost, opened, phases, partner, periodic, table,
    load_sem, coef_sem, core_send, core_recv, near_send, near_recv, far_send, far_recv, row_send, row_recv,
    axial_send, axial_recv, pitch_send, pitch_recv, span_send, span_recv, ready, span_ready,
):
    n_axial, n_pitch, n_span, n_var, n_row, n_col, n_cell, n_term = sizes
    at = lax.axis_index("axial")
    pitch = lax.axis_index("pitch")
    span = lax.axis_index("span")
    chips = n_pitch // 2
    n_z = min(n_axial, 8)
    core = lax.rem(pitch, 2)
    chip = lax.div(pitch, 2)
    place = jnp.where(core == 0, chips - 1 - chip, chip)
    toward = 1 - 2 * core
    is_end = place == chips - 1
    is_helper = place == chips - 2
    is_middle = place == chips - 3
    is_start = place == chips - 4
    end = jnp.where(core == 0, 0, n_pitch - 1)
    helper = end + 2 * toward
    middle = end + 4 * toward
    mate = pitch + 1 - 2 * core
    beside = pitch - 1 + 2 * core
    has_beside = (beside >= 0) & (beside < n_pitch)
    tail = n_cell - LANES
    first_blade, end_blade = n_axial // 4, 3 * n_axial // 4

    def is_blade(a):
        return (a >= first_blade) & (a < end_blade)

    def load_coef(face, v):
        source = upper_coef if face == 0 else lower_coef
        return pltpu.make_async_copy(source.at[:, v], coef.at[face, :, v], coef_sem.at[face, v])

    def wait_coef(mine, v):
        pl.when(core == 0)(lambda: load_coef(0 if mine else 1, v).wait())
        pl.when(core == 1)(lambda: load_coef(1 if mine else 0, v).wait())

    load_flow = pltpu.make_async_copy(flow, fx.at[:, pl.ds(1, n_row)], load_sem.at[2])
    load_step = pltpu.make_async_copy(step, sx, load_sem.at[3])
    load_phases = pltpu.make_async_copy(phases_in, phases, load_sem.at[4])
    load_partner = pltpu.make_async_copy(partner_in, partner, load_sem.at[5])
    load_periodic = pltpu.make_async_copy(periodic_in, periodic, load_sem.at[6])
    load_phases.start()
    for first in range(2):

        @pl.when(core == first)
        def _():
            for face in (1 - first, first):
                for v in range(n_var):
                    load_coef(face, v).start()

    load_partner.start()
    load_periodic.start()

    barrier = pltpu.get_barrier_semaphore()

    def greet(**where):
        pl.semaphore_signal(barrier, inc=1, device_id=where, device_id_type=MESH)

    one = jnp.int32(1)
    zero = jnp.int32(0)

    def tell(sem, **where):
        pl.semaphore_signal(sem, inc=1, device_id=where, device_id_type=MESH)

    @pl.when(is_end)
    def _():
        @pl.loop(1, n_axial)
        def _(j):
            greet(axial=lax.rem(at + j, n_axial), pitch=helper)

    pl.when(is_end)(lambda: greet(pitch=helper))
    pl.when(is_end)(lambda: greet(pitch=middle))
    pl.when(is_middle)(lambda: greet(pitch=pitch + 2 * toward))
    greetings = jnp.where(is_helper, n_axial - 1, zero) + jnp.where(is_end, zero, one)
    greet(span=1 - span, pitch=jnp.where(span == 1, n_pitch - 3, 2))
    collector = jnp.where(span == 0, n_pitch - 3, 2)
    is_collector = pitch == collector
    pl.when(jnp.logical_not(is_collector))(lambda: greet(pitch=collector))
    greetings = greetings + jnp.where(is_collector, 2 * n_pitch - 1, zero)
    for holds, where in (
        (None, {"pitch": mate}),
        (has_beside, {"pitch": beside}),
        (at > 0, {"axial": at - 1}),
        (at < n_axial - 1, {"axial": at + 1}),
    ):
        if holds is None:
            greet(**where)
            greetings = greetings + 1
        else:
            pl.when(holds)(functools.partial(greet, **where))
            greetings = greetings + jnp.where(holds, one, zero)

    load_phases.wait()
    spot = lax.broadcasted_iota(jnp.int32, (8, LANES), 1)
    second = spot >= n_term
    term = pitch * n_term + jnp.where(second, spot - n_term, spot)
    angle = lax.shift_right_logical(term + 1, 1).astype(jnp.float32) * jnp.where(second, phases[1], phases[0])
    basis = jnp.where((lax.rem(term, 2) == 0) & (term > 0), jnp.sin(angle), jnp.cos(angle))

    def evaluate(face, v):
        first = jnp.where(face == 0, basis, pltpu.roll(basis, LANES - n_term, 1))
        value = first[:1, :1] * coef[face, 0, v]
        for t in range(1, n_term):
            value = value + first[:1, t : t + 1] * coef[face, t, v]
        part[face, v] = value

    def core_copy(v):
        return pltpu.make_async_remote_copy(
            src_ref=part.at[1 - core, v], dst_ref=rx_core.at[v], send_sem=core_send.at[v], recv_sem=core_recv.at[v],
            device_id={"pitch": mate}, device_id_type=MESH)

    pl.semaphore_wait(barrier, greetings)
    for v in range(n_var):
        wait_coef(False, v)
        evaluate(1 - core, v)
        core_copy(v).start()

    load_flow.start()
    pl.when(is_helper)(lambda: tell(ready, pitch=end))

    @pl.when(is_collector)
    def _():
        for k in range(n_pitch):
            pl.when(pitch != k)(lambda: tell(span_ready, pitch=k))

    for v in range(n_var):
        wait_coef(True, v)
        evaluate(core, v)

    load_step.start()

    def near_copy(v):
        return pltpu.make_async_remote_copy(
            src_ref=total.at[v], dst_ref=rx_near.at[v], send_sem=near_send.at[v], recv_sem=near_recv.at[v],
            device_id={"pitch": pitch - 2 * toward}, device_id_type=MESH)

    def far_copy(v):
        return pltpu.make_async_remote_copy(
            src_ref=total.at[v], dst_ref=rx_far.at[v], send_sem=far_send.at[v], recv_sem=far_recv.at[v],
            device_id={"pitch": end}, device_id_type=MESH)

    for v in range(n_var):
        core_copy(v).wait_recv()
        total[v] = part[core, v] + rx_core[v]
        pl.when(is_start | is_helper)(lambda: near_copy(v).start())

    if chips > 2:
        @pl.when(is_middle)
        def _():
            for v in range(n_var):
                if chips > 3:
                    near_copy(v).wait_recv()
                    total[v] = total[v] + rx_near[v]
                far_copy(v).start()
    load_flow.wait()

    def axial_up():
        return pltpu.make_async_remote_copy(
            src_ref=fx.at[:, n_row], dst_ref=fx.at[:, 0], send_sem=axial_send.at[0], recv_sem=axial_recv.at[0],
            device_id={"axial": at + 1}, device_id_type=MESH)

    def axial_down():
        return pltpu.make_async_remote_copy(
            src_ref=fx.at[:, 1], dst_ref=fx.at[:, n_row + 1], send_sem=axial_send.at[1], recv_sem=axial_recv.at[1],
            device_id={"axial": at - 1}, device_id_type=MESH)

    @pl.when(at < n_axial - 1)
    def _():
        axial_up().start()

    @pl.when(at > 0)
    def _():
        axial_down().start()

    lane = lax.broadcasted_iota(jnp.int32, (n_col, LANES), 1)
    span_copy = pltpu.make_async_remote_copy(
        src_ref=span_tx, dst_ref=span_rx, send_sem=span_send, recv_sem=span_recv,
        device_id={"span": 1 - span}, device_id_type=MESH)

    def pitch_up():
        return pltpu.make_async_remote_copy(
            src_ref=edge.at[1], dst_ref=halo.at[0], send_sem=pitch_send.at[0], recv_sem=pitch_recv.at[0],
            device_id={"pitch": pitch + 1}, device_id_type=MESH)

    def pitch_down():
        return pltpu.make_async_remote_copy(
            src_ref=edge.at[0], dst_ref=halo.at[1], send_sem=pitch_send.at[1], recv_sem=pitch_recv.at[1],
            device_id={"pitch": pitch - 1}, device_id_type=MESH)

    def pack(i, carry):
        low, high = carry
        for v in range(n_var):
            spot = v * n_row + i
            last = pltpu.roll(fx[v, i + 1, :, pl.ds(tail, LANES)], spot + 1, 1)
            first = pltpu.roll(fx[v, i + 1, :, pl.ds(0, LANES)], spot, 1)
            low = jnp.where(lane == spot, last, low)
            high = jnp.where(lane == spot, first, high)
        return low, high

    def send_edges():
        blank = jnp.ones((n_col, LANES), jnp.float32)
        low, high = lax.fori_loop(0, n_row, pack, (blank, blank))
        span_tx[0] = low
        span_tx[1] = high
        pl.when(is_collector)(lambda: span_copy.start())

        @pl.loop(0, n_row)
        def _(i):
            for v in range(n_var):
                edge[0, v, pl.ds(i, 1), :] = fx[v, i + 1, pl.ds(0, 1), :]
                edge[1, v, pl.ds(i, 1), :] = fx[v, i + 1, pl.ds(n_col - 1, 1), :]

        pl.when(core == 0)(lambda: pitch_up().start())
        pl.when(core == 1)(lambda: pitch_down().start())
        pl.when((core == 0) & (pitch > 0))(lambda: pitch_down().start())
        pl.when((core == 1) & (pitch < n_pitch - 1))(lambda: pitch_up().start())

    def send_span():
        pl.semaphore_wait(span_ready, 1)
        span_copy.start()

    send_edges()


    load_partner.wait()
    load_periodic.wait()

    @pl.when(is_end)
    def _():
        @pl.loop(0, n_axial)
        def _(d):
            index = jnp.int32(0)
            for r in range(n_row):
                index = jnp.where(lax.div(partner[1 - core, r], n_row) == d, r, index)
            table[d] = index

    pl.when(jnp.logical_not(is_collector))(send_span)

    def row_copy(target):
        return pltpu.make_async_remote_copy(
            src_ref=slots.at[target], dst_ref=recv.at[at], send_sem=row_send, recv_sem=row_recv,
            device_id={"axial": target}, device_id_type=MESH)

    def tip_copy(target):
        return pltpu.make_async_remote_copy(
            src_ref=slots.at[target, :, :, pl.ds(tail, LANES)], dst_ref=recv.at[at, :, :, pl.ds(tail, LANES)],
            send_sem=row_send, recv_sem=row_recv, device_id={"axial": target}, device_id_type=MESH)

    @pl.when(is_end)
    def _():
        for v in range(n_var):
            near_copy(v).wait_recv()
            total[v] = total[v] + rx_near[v]
            if chips > 2:
                far_copy(v).wait_recv()
                total[v] = total[v] + rx_far[v]

            @pl.loop(0, n_axial, unroll=4)
            def _(d):
                slots[d, v] = total[v, pl.ds(table[d], 1), :]

        pl.semaphore_wait(ready, 1)

        order = sorted(range(n_axial), key=lambda d: (first_blade <= d < end_blade, d % n_z))
        for target in order:
            if first_blade <= target < end_blade:
                pl.when((at != target) & (span == n_span - 1))(lambda: tip_copy(target).start())
            else:
                pl.when(at != target)(lambda: row_copy(target).start())

        own = table[at]
        for v in range(n_var):
            recv[at, v] = total[v, pl.ds(own, 1), :]

    load_step.wait()
    cell = lax.broadcasted_iota(jnp.int32, (n_col, n_cell), 1)
    col = lax.broadcasted_iota(jnp.int32, (n_col, n_cell), 0)

    def stencil(i, carry):
        before = [fx[v, i] for v in range(n_var)]
        after = [fx[v, i + 2] for v in range(n_var)]
        flux_before = flux_of(before, pressure_of(before), 1)
        flux_after = flux_of(after, pressure_of(after), 1)
        for v in range(n_var):
            out_v[v, i] = sx[v, i] + 0.125 * (before[v] + after[v]) + 0.25 * (flux_before[v] - flux_after[v])
        u = [fx[v, i + 1] for v in range(n_var)]
        p = pressure_of(u)
        flux = flux_of(u, p, 2)
        above = as_next(u, flux)
        below = as_previous(u, flux)
        for v in range(n_var):
            down = jnp.where(col == 0, 0.0, pltpu.roll(below[v], 1, 0))
            up = jnp.where(col == n_col - 1, 0.0, pltpu.roll(above[v], n_col - 1, 0))
            out_v[v, i] = out_v[v, i] + down + up - 0.75 * u[v]
        flux = flux_of(u, p, 3)
        above = as_next(u, flux)
        below = as_previous(u, flux)
        for v in range(n_var):
            down = jnp.where(cell == 0, 0.0, pltpu.roll(below[v], 1, 1))
            up = jnp.where(cell == n_cell - 1, 0.0, pltpu.roll(above[v], n_cell - 1, 1))
            out_v[v, i] = out_v[v, i] + down + up
        return carry

    lax.fori_loop(1, n_row - 1, stencil, 0)


    @pl.when(at > 0)
    def _():
        axial_up().wait_recv()

    @pl.when(at == 0)
    def _():
        for v in range(n_var):
            fx[v, 0] = fx[v, 1]

    @pl.when(at < n_axial - 1)
    def _():
        axial_down().wait_recv()

    @pl.when(at == n_axial - 1)
    def _():
        for v in range(n_var):
            fx[v, n_row + 1] = fx[v, n_row]

    lax.fori_loop(0, 2, lambda k, carry: stencil(k * (n_row - 1), carry), 0)

    span_copy.wait_recv()
    for side, form in enumerate((as_previous, as_next)):
        u = [span_rx[side]]
        for v in range(1, n_var):
            u.append(pltpu.roll(span_rx[side], LANES - v * n_row, 1))
        for v, value in enumerate(form(u, flux_of(u, pressure_of(u), 3))):
            span_in[side, v] = value

    def add_span(i, carry):
        for v in range(n_var):
            first = jnp.where(lane == 0, pltpu.roll(span_in[0, v], LANES - i, 1), 0.0)
            last = jnp.where(lane == LANES - 1, pltpu.roll(span_in[1, v], LANES - 1 - i, 1), 0.0)
            out_v[v, i, :, pl.ds(0, LANES)] = out_v[v, i, :, pl.ds(0, LANES)] + first
            out_v[v, i, :, pl.ds(tail, LANES)] = out_v[v, i, :, pl.ds(tail, LANES)] + last
        return carry

    lax.fori_loop(0, n_row, add_span, 0)


    def add_side(side, u):
        form = (as_previous, as_next)[side]
        for v, value in enumerate(form(u, flux_of(u, pressure_of(u), 2))):
            sides[side, v] = value

    @pl.when(pitch > 0)
    def _():
        pitch_up().wait_recv()
        add_side(0, [halo[0, v] for v in range(n_var)])

    @pl.when(pitch < n_pitch - 1)
    def _():
        pitch_down().wait_recv()
        add_side(1, [halo[1, v] for v in range(n_var)])

    @pl.when(is_end)
    def _():
        blade = is_blade(at)
        position = lax.broadcasted_iota(jnp.int32, (1, n_cell), 1) + span * n_cell
        for i in range(n_row):
            opened[pl.ds(i, 1), :] = jnp.where(position >= n_span * n_cell - periodic[core, i], 1.0, 0.0)

        @pl.when(jnp.logical_not(blade))
        def _():
            pltpu.make_async_copy(
                slots.at[pl.ds(0, n_axial - 1)], recv.at[pl.ds(0, n_axial - 1)], row_recv).wait()

        @pl.when(blade & (span == n_span - 1))
        def _():
            pltpu.make_async_copy(
                slots.at[pl.ds(0, n_axial - 1), :, :, pl.ds(tail, LANES)],
                recv.at[pl.ds(0, n_axial - 1), :, :, pl.ds(tail, LANES)], row_recv).wait()

        for i in range(n_row):
            source = lax.div(partner[core, i], n_row)
            for v in range(n_var):
                ghost[v, pl.ds(i, 1), :] = recv[source, v]

        is_open = opened[...] > 0.5
        u = []
        for v in range(n_var):
            wall = edge[core, v]
            u.append(jnp.where(is_open, ghost[v], -wall if v == 2 else wall))
        pl.when(core == 0)(lambda: add_side(0, u))
        pl.when(core == 1)(lambda: add_side(1, u))

    for v in range(n_var):
        core_copy(v).wait_send()

    @pl.when(is_start | is_helper)
    def _():
        for v in range(n_var):
            near_copy(v).wait_send()

    if chips > 2:
        @pl.when(is_middle)
        def _():
            for v in range(n_var):
                far_copy(v).wait_send()

    @pl.when(is_end)
    def _():
        @pl.loop(1, n_axial)
        def _(j):
            target = lax.rem(at + j, n_axial)

            @pl.when(jnp.logical_not(is_blade(target)))
            def _():
                row_copy(target).wait_send()

            @pl.when(is_blade(target) & (span == n_span - 1))
            def _():
                tip_copy(target).wait_send()

    @pl.when(at < n_axial - 1)
    def _():
        axial_up().wait_send()

    @pl.when(at > 0)
    def _():
        axial_down().wait_send()

    @pl.when(pitch < n_pitch - 1)
    def _():
        pitch_up().wait_send()

    @pl.when(pitch > 0)
    def _():
        pitch_down().wait_send()

    span_copy.wait_send()


def join(acc, sides, out, stage, sem):
    n_var, n_row, n_col, n_cell = acc.shape
    col = lax.broadcasted_iota(jnp.int32, (n_col, n_cell), 0)

    def put(v):
        return pltpu.make_async_copy(stage.at[v], out.at[v], sem.at[v])

    for v in range(n_var):
        for i in range(n_row):
            low, high = (jnp.where(col == e, sides[k, v, pl.ds(i, 1), :], 0.0) for k, e in ((0, 0), (1, n_col - 1)))
            stage[v, i] = acc[v, i] + low + high
        put(v).start()
    for v in range(n_var):
        put(v).wait()


def per_device(flow, step, lower_coef, upper_coef, partner, periodic, phase_angles):
    n_axial = lax.axis_size("axial")
    n_pitch = lax.axis_size("pitch")
    n_span = lax.axis_size("span")
    n_var, n_row, n_col, n_cell = flow.shape
    n_term = lower_coef.shape[0]
    sizes = (n_axial, n_pitch, n_span, n_var, n_row, n_col, n_cell, n_term)
    any_spec = pl.BlockSpec(memory_space=pl.ANY)
    vmem = pl.BlockSpec(memory_space=pltpu.VMEM)
    face = (n_var, n_row, n_cell)
    f32 = jnp.float32
    dma = pltpu.SemaphoreType.DMA
    flow, step, lower_coef, upper_coef, phase_angles, partner, periodic = (
        pltpu.with_memory_space_constraint(a, pltpu.HBM)
        for a in (flow, step, lower_coef, upper_coef, phase_angles, partner, periodic))
    acc, sides = pl.pallas_call(
        functools.partial(kernel, sizes),
        out_shape=(pltpu.VMEM(flow.shape, f32), pltpu.VMEM((2, *face), f32)),
        in_specs=[any_spec] * 7,
        out_specs=(vmem, vmem),
        scratch_shapes=[
            pltpu.VMEM((n_var, n_row + 2, n_col, n_cell), f32),
            pltpu.VMEM(flow.shape, f32),
            pltpu.VMEM((2, n_term, *face), f32),
            pltpu.VMEM((2, *face), f32),
            pltpu.VMEM(face, f32),
            pltpu.VMEM(face, f32),
            pltpu.VMEM(face, f32),
            pltpu.VMEM(face, f32),
            pltpu.VMEM((n_axial, n_var, 1, n_cell), f32),
            pltpu.VMEM((n_axial, n_var, 1, n_cell), f32),
            pltpu.VMEM((2, *face), f32),
            pltpu.VMEM((2, *face), f32),
            pltpu.VMEM((2, n_col, LANES), f32),
            pltpu.VMEM((2, n_col, LANES), f32),
            pltpu.VMEM((2, n_var, n_col, LANES), f32),
            pltpu.VMEM(face, f32),
            pltpu.VMEM(face[1:], f32),
            pltpu.SMEM(phase_angles.shape, f32),
            pltpu.SMEM(partner.shape, jnp.int32),
            pltpu.SMEM(periodic.shape, jnp.int32),
            pltpu.SMEM((n_axial,), jnp.int32),
            dma((7,)), dma((2, n_var)), dma((n_var,)), dma((n_var,)), dma((n_var,)), dma((n_var,)),
            dma((n_var,)), dma((n_var,)), dma, dma, dma((2,)), dma((2,)), dma((2,)), dma((2,)), dma, dma,
            pltpu.SemaphoreType.REGULAR, pltpu.SemaphoreType.REGULAR,
        ],
        compiler_params=pltpu.CompilerParams(collective_id=0, has_side_effects=True, vmem_limit_bytes=24 << 20),
        name="section",
    )(flow, step, lower_coef, upper_coef, phase_angles, partner, periodic)
    acc, sides = (pltpu.with_memory_space_constraint(a, pltpu.VMEM) for a in (acc, sides))
    return pl.pallas_call(
        join,
        out_shape=jax.ShapeDtypeStruct(flow.shape, f32),
        in_specs=[vmem, vmem],
        out_specs=any_spec,
        scratch_shapes=[pltpu.VMEM(flow.shape, f32), dma((n_var,))],
        compiler_params=pltpu.CompilerParams(vmem_limit_bytes=8 << 20),
        name="join",
    )(acc, sides)


def solution(mesh):
    in_specs = (
        P(None, "axial", "pitch", "span"),
        P(None, "axial", "pitch", "span"),
        P("pitch", None, "axial", "span"),
        P("pitch", None, "axial", "span"),
        P(None, "axial"),
        P(None, "axial"),
        P(),
    )
    out_specs = P(None, "axial", "pitch", "span")
    return jax.shard_map(
        per_device, mesh=mesh, in_specs=in_specs, out_specs=out_specs, check_vma=False
    )
```
